256 devices in a mesh: fsdp: 32 (over z, x_hi, core), tp: 8 (over x_lo, y).
Axes of the slice: x: 4 (x_hi: 2, x_lo: 2; x = x_hi * 2 + x_lo), y: 4, z: 8, core: 2. Of those that a mesh axis runs over, the one named last changes fastest.
Arguments:
- grad_iterate: bfloat16 [3584, 18432], P('tp', 'fsdp'), may hold values from -0.036828478 to 0.036828478
Outputs:
- update: float32 [3584, 18432], P('tp', 'fsdp')
The draws below stay inside these ranges and needn't reach their ends.
All inputs are finite; a program needn't handle non-finite values.
Results may differ from the reference program's by a relative error of at most 0.0031.
Values may be sent and summed in bfloat16 or wider, within the bound.
No kernel may reach another device: no remote copies, remote signals or barrier semaphores. Data moves between devices by JAX's collectives and lax.ppermute only.
A program may use at most 64 MiB of HBM per device.

```python
import math
import jax
import jax.numpy as jnp

R = 3584
C = 18432


def draw_grad_iterate(key, part):
    key_one = jax.random.fold_in(key, 11)
    key_two = jax.random.fold_in(key, 23)
    key_four = jax.random.fold_in(key, 41)
    key_five = jax.random.fold_in(key, 53)
    key_six = jax.random.fold_in(key, 67)
    shared_rank = max(R // 4, 1)
    row_scale = jnp.exp(jax.random.uniform(key_two, (R, 1), jnp.float32, math.log(0.1), 0.0))
    factor_gain = jnp.exp(jax.random.uniform(key_six, (1, shared_rank), jnp.float32, math.log(0.4), math.log(1.6)))
    factor_gain = factor_gain / jnp.sqrt(jnp.mean(factor_gain * factor_gain))
    left_factor = jax.random.normal(key_four, (R, shared_rank), jnp.float32) * factor_gain
    right_factor = jax.random.normal(key_five, (shared_rank, C), jnp.float32)
    shared = jnp.dot(left_factor, right_factor) / math.sqrt(shared_rank)
    noise = jax.random.normal(key_one, (R, C), jnp.float32)
    entries = jnp.clip(0.25 * noise + 0.9 * shared, -3.5, 3.5)
    return (entries * row_scale / math.sqrt(C)).astype(jnp.bfloat16)


def setup_inputs(seed: int = 0) -> dict:
    arg_keys = jax.random.split(jax.random.key(seed), 2)
    return {
        "grad_iterate": draw_grad_iterate(jax.random.fold_in(arg_keys[1], 71), 0),
    }


quintic_one = 3.4445
quintic_three = -4.775
quintic_five = 2.0315

def reference(grad_iterate):
    gram = jnp.dot(grad_iterate, grad_iterate.T, preferred_element_type=jnp.float32)
    gram_low = gram.astype(jnp.bfloat16)
    applied = jnp.dot(gram_low, grad_iterate, preferred_element_type=jnp.float32)
    applied_low = applied.astype(jnp.bfloat16)
    twice_applied = jnp.dot(gram_low, applied_low, preferred_element_type=jnp.float32)
    mixed = quintic_one * grad_iterate.astype(jnp.float32) + quintic_three * applied + quintic_five * twice_applied
    return mixed * math.sqrt(C)
```

```python
import math

import jax
import jax.numpy as jnp
from jax import lax
from jax.sharding import Mesh, PartitionSpec as P

C = 18432


quintic_one = 3.4445
quintic_three = -4.775
quintic_five = 2.0315

TP = ("x_lo", "y")
SWAP = [(0, 1), (1, 0)]


def dot(a, b, dims):
    return lax.dot_general(a, b, (dims, ((), ())), preferred_element_type=jnp.float32)


def local(x):
    core = lax.axis_index("core")
    columns = lax.all_gather(x, TP, axis=0, tiled=True)
    half = columns.shape[0] // 2
    mine = lax.dynamic_slice_in_dim(columns, core * half, half, 0)
    other = lax.dynamic_slice_in_dim(columns, (1 - core) * half, half, 0)
    got = lax.ppermute(dot(x, other, ((1,), (1,))), "core", SWAP)
    pair = dot(x, mine, ((1,), (1,))) + got
    rows = lax.psum_scatter(pair, "z", scatter_dimension=0, tiled=True)
    rows = rows + lax.ppermute(rows, "x_hi", SWAP)
    gram_mine = lax.all_gather(rows.astype(jnp.bfloat16), "z", axis=0, tiled=True)
    gram_other = lax.ppermute(gram_mine, "core", SWAP)
    applied = dot(gram_mine, mine, ((1,), (0,))) + dot(gram_other, other, ((1,), (0,)))
    applied_all = lax.all_gather(applied.astype(jnp.bfloat16), TP, axis=0, tiled=True)
    applied_mine = lax.dynamic_slice_in_dim(applied_all, core * half, half, 0)
    applied_other = lax.dynamic_slice_in_dim(applied_all, (1 - core) * half, half, 0)
    twice_applied = dot(gram_mine, applied_mine, ((1,), (0,))) + dot(
        gram_other, applied_other, ((1,), (0,))
    )
    mixed = (
        quintic_one * x.astype(jnp.float32)
        + quintic_three * applied
        + quintic_five * twice_applied
    )
    return mixed * math.sqrt(C)


def solution(mesh):
    grid = Mesh(mesh.devices.reshape(8, 2, 2, 2, 4), ("z", "x_hi", "core", "x_lo", "y"))
    spec = P(TP, ("z", "x_hi", "core"))
    return jax.shard_map(local, mesh=grid, in_specs=(spec,), out_specs=spec, check_vma=False)
```

```python
import math

import jax
import jax.numpy as jnp
from jax import lax
from jax.sharding import Mesh, PartitionSpec as P

C = 18432


quintic_one = 3.4445
quintic_three = -4.775
quintic_five = 2.0315

TP = ("x_lo", "y")
SWAP = [(0, 1), (1, 0)]


def dot(a, b, dims):
    return lax.dot_general(a, b, (dims, ((), ())), preferred_element_type=jnp.float32)


def shift(v, axis, size, by):
    return lax.ppermute(v, axis, [(i, (i + by) % size) for i in range(size)])


def swap(v, axis):
    return lax.ppermute(v, axis, SWAP)


def gather_tp(first, second):
    h = second.shape[0] // 2
    s_left = shift(second, "y", 4, 1)
    s_right = shift(second, "y", 4, -1)
    f_x = swap(first, "x_lo")
    s_x = swap(second, "x_lo")
    f_left = shift(first, "y", 4, 1)
    f_right = shift(first, "y", 4, -1)
    s_far = jnp.concatenate([shift(s_left[:h], "y", 4, 1), shift(s_right[h:], "y", 4, -1)], axis=0)
    fx_left = shift(f_x, "y", 4, 1)
    fx_right = shift(f_x, "y", 4, -1)
    sx_left = swap(s_left, "x_lo")
    sx_right = swap(s_right, "x_lo")
    f_far = shift(f_left, "y", 4, 1)
    fx_far = shift(fx_right, "y", 4, -1)
    sx_far = swap(s_far, "x_lo")
    firsts = [first, f_x, f_left, fx_left, f_right, fx_right, f_far, fx_far]
    seconds = [second, s_x, s_left, sx_left, s_right, sx_right, s_far, sx_far]
    firsts, seconds = lax.optimization_barrier((firsts, seconds))
    return jnp.concatenate(firsts, axis=0), jnp.concatenate(seconds, axis=0)


def gather_z(v):
    rows, columns = v.shape
    h = columns // 2
    z = lax.axis_index("z")
    r1 = shift(v, "z", 8, 1)
    l1 = shift(v, "z", 8, -1)
    r2 = shift(v, "z", 8, 2)
    l2 = shift(v, "z", 8, -2)
    r3 = shift(r1, "z", 8, 2)
    l3 = shift(l1, "z", 8, -2)
    far = jnp.concatenate([shift(r3[:, :h], "z", 8, 1), shift(l3[:, h:], "z", 8, -1)], axis=1)
    out = jnp.zeros((8 * rows, columns), v.dtype)
    for by, piece in ((0, v), (-1, r1), (1, l1), (-2, r2), (2, l2), (-3, r3), (3, l3), (4, far)):
        out = lax.dynamic_update_slice_in_dim(out, piece, lax.rem(z + by + 8, 8) * rows, 0)
    return out


def halves(v, core):
    half = v.shape[0] // 2
    return (
        lax.dynamic_slice_in_dim(v, core * half, half, 0),
        lax.dynamic_slice_in_dim(v, (1 - core) * half, half, 0),
    )


def local(x):
    core = lax.axis_index("core")
    mine, other = gather_tp(*halves(x, core))
    got = swap(dot(x, other, ((1,), (1,))), "core")
    pair = dot(x, mine, ((1,), (1,))) + got
    rows = lax.psum_scatter(pair, "z", scatter_dimension=0, tiled=True)
    rows = rows + swap(rows, "x_hi")
    gram_mine = gather_z(rows.astype(jnp.bfloat16))
    gram_other = swap(gram_mine, "core")
    applied = dot(gram_mine, mine, ((1,), (0,))) + dot(gram_other, other, ((1,), (0,)))
    applied_mine, applied_other = gather_tp(*halves(applied.astype(jnp.bfloat16), core))
    twice_applied = dot(gram_mine, applied_mine, ((1,), (0,))) + dot(
        gram_other, applied_other, ((1,), (0,))
    )
    mixed = (
        quintic_one * x.astype(jnp.float32)
        + quintic_three * applied
        + quintic_five * twice_applied
    )
    return mixed * math.sqrt(C)


def solution(mesh):
    grid = Mesh(mesh.devices.reshape(8, 2, 2, 2, 4), ("z", "x_hi", "core", "x_lo", "y"))
    spec = P(TP, ("z", "x_hi", "core"))
    return jax.shard_map(local, mesh=grid, in_specs=(spec,), out_specs=spec, check_vma=False)
```

```python
import math

import jax
import jax.numpy as jnp
from jax import lax
from jax.sharding import Mesh, PartitionSpec as P

C = 18432


quintic_one = 3.4445
quintic_three = -4.775
quintic_five = 2.0315

TP = ("x_lo", "y")
SWAP = [(0, 1), (1, 0)]


def dot(a, b, dims):
    return lax.dot_general(a, b, (dims, ((), ())), preferred_element_type=jnp.float32)


def shift(v, axis, size, by):
    return lax.ppermute(v, axis, [(i, (i + by) % size) for i in range(size)])


def swap(v, axis):
    return lax.ppermute(v, axis, SWAP)


def gather_tp(first, second):
    h = second.shape[0] // 2
    s_left = shift(second, "y", 4, 1)
    s_right = shift(second, "y", 4, -1)
    f_x = swap(first, "x_lo")
    s_x = swap(second, "x_lo")
    f_left = shift(first, "y", 4, 1)
    f_right = shift(first, "y", 4, -1)
    f_early, s_early = lax.optimization_barrier(
        ([first, f_x, f_left, f_right], [second, s_x, s_left, s_right])
    )
    s_far = jnp.concatenate([shift(s_left[:h], "y", 4, 1), shift(s_right[h:], "y", 4, -1)], axis=0)
    fx_left = shift(f_x, "y", 4, 1)
    fx_right = shift(f_x, "y", 4, -1)
    sx_left = swap(s_left, "x_lo")
    sx_right = swap(s_right, "x_lo")
    f_far = shift(f_left, "y", 4, 1)
    fx_far = shift(fx_right, "y", 4, -1)
    sx_far = swap(s_far, "x_lo")
    f_late, s_late = lax.optimization_barrier(
        ([fx_left, fx_right, f_far, fx_far], [sx_left, sx_right, s_far, sx_far])
    )
    return [tuple(jnp.concatenate(v, axis=0) for v in part) for part in ((f_early, s_early), (f_late, s_late))]


def gather_z(v, base):
    rows, columns = v.shape
    h = columns // 2
    z = lax.axis_index("z")
    r1 = shift(v, "z", 8, 1)
    l1 = shift(v, "z", 8, -1)
    r2 = shift(v, "z", 8, 2)
    l2 = shift(v, "z", 8, -2)
    r3 = shift(r1, "z", 8, 2)
    l3 = shift(l1, "z", 8, -2)
    far = jnp.concatenate([shift(r3[:, :h], "z", 8, 1), shift(l3[:, h:], "z", 8, -1)], axis=1)
    out = base
    for by, piece in ((0, v), (-1, r1), (1, l1), (-2, r2), (2, l2), (-3, r3), (3, l3), (4, far)):
        out = lax.dynamic_update_slice_in_dim(out, piece, lax.rem(z + by + 8, 8) * rows, 0)
    return out


def halves(v, core):
    half = v.shape[0] // 2
    return (
        lax.dynamic_slice_in_dim(v, core * half, half, 0),
        lax.dynamic_slice_in_dim(v, (1 - core) * half, half, 0),
    )


def low(v):
    return v.astype(jnp.bfloat16)


def wide(v):
    return v.astype(jnp.float32)


def local(x):
    core = lax.axis_index("core")
    parts = gather_tp(*halves(x, core))
    rows = []
    for mine, other in parts:
        got = swap(low(dot(x, other, ((1,), (1,)))), "core")
        pair = low(dot(x, mine, ((1,), (1,))) + wide(got))
        split = pair.reshape(8, pair.shape[0] // 8, pair.shape[1])
        split = lax.all_to_all(split, "z", 0, 0)
        plane = low(jnp.sum(wide(split), axis=0))
        rows.append(low(wide(plane) + wide(swap(plane, "x_hi"))))
    rows = jnp.concatenate(rows, axis=1)
    gram_mine = gather_z(rows, jnp.zeros((8 * rows.shape[0], rows.shape[1]), rows.dtype))
    gram_other = swap(gram_mine, "core")
    n = rows.shape[1] // 2
    grams = [(gram_mine[:, :n], gram_other[:, :n]), (gram_mine[:, n:], gram_other[:, n:])]

    def apply(blocks):
        total = 0
        for gram, block in zip(grams, blocks):
            for g, b in zip(gram, block):
                total = total + dot(g, b, ((1,), (0,)))
        return total

    applied = apply(parts)
    twice_applied = apply(gather_tp(*halves(low(applied), core)))
    mixed = (
        quintic_one * x.astype(jnp.float32)
        + quintic_three * applied
        + quintic_five * twice_applied
    )
    return mixed * math.sqrt(C)


def solution(mesh):
    grid = Mesh(mesh.devices.reshape(8, 2, 2, 2, 4), ("z", "x_hi", "core", "x_lo", "y"))
    spec = P(TP, ("z", "x_hi", "core"))
    return jax.shard_map(local, mesh=grid, in_specs=(spec,), out_specs=spec, check_vma=False)
```

```python
import math

import jax
import jax.numpy as jnp
from jax import lax
from jax.sharding import Mesh, PartitionSpec as P

C = 18432


quintic_one = 3.4445
quintic_three = -4.775
quintic_five = 2.0315

TP = ("x_lo", "y")
SWAP = [(0, 1), (1, 0)]


def dot(a, b, dims):
    return lax.dot_general(a, b, (dims, ((), ())), preferred_element_type=jnp.float32)


def shift(v, axis, size, by):
    return lax.ppermute(v, axis, [(i, (i + by) % size) for i in range(size)])


def swap(v, axis):
    return lax.ppermute(v, axis, SWAP)


def gather_tp(first, second, early_work=None):
    h = second.shape[0] // 2
    s_left = shift(second, "y", 4, 1)
    s_right = shift(second, "y", 4, -1)
    f_x = swap(first, "x_lo")
    s_x = swap(second, "x_lo")
    f_left = shift(first, "y", 4, 1)
    f_right = shift(first, "y", 4, -1)
    s_far = jnp.concatenate([shift(s_left[:h], "y", 4, 1), shift(s_right[h:], "y", 4, -1)], axis=0)
    fx_left = shift(f_x, "y", 4, 1)
    fx_right = shift(f_x, "y", 4, -1)
    sx_left = swap(s_left, "x_lo")
    sx_right = swap(s_right, "x_lo")
    early = (
        jnp.concatenate([first, f_x, f_left, f_right], axis=0),
        jnp.concatenate([second, s_x, s_left, s_right], axis=0),
    )
    hops = (f_left, fx_right, s_far)
    if early_work is not None:
        prepare, send = early_work
        prepared, hops = lax.optimization_barrier((prepare(early), hops))
        sent = send(prepared)
    f_far = shift(hops[0], "y", 4, 1)
    fx_far = shift(hops[1], "y", 4, -1)
    sx_far = swap(hops[2], "x_lo")
    lates = ([fx_left, fx_right, f_far, fx_far], [sx_left, sx_right, s_far, sx_far])
    if early_work is not None:
        sent, lates = lax.optimization_barrier((sent, lates))
    late = tuple(jnp.concatenate(v, axis=0) for v in lates)
    if early_work is not None:
        return (early, late), sent
    return early, late


def gather_z(v, base):
    rows, columns = v.shape
    h = columns // 2
    z = lax.axis_index("z")
    r1 = shift(v, "z", 8, 1)
    l1 = shift(v, "z", 8, -1)
    r2 = shift(v, "z", 8, 2)
    l2 = shift(v, "z", 8, -2)
    r3 = shift(r1, "z", 8, 2)
    l3 = shift(l1, "z", 8, -2)
    far = jnp.concatenate([shift(r3[:, :h], "z", 8, 1), shift(l3[:, h:], "z", 8, -1)], axis=1)
    out = base
    for by, piece in ((0, v), (-1, r1), (1, l1), (-2, r2), (2, l2), (-3, r3), (3, l3), (4, far)):
        out = lax.dynamic_update_slice_in_dim(out, piece, lax.rem(z + by + 8, 8) * rows, 0)
    return out


def halves(v, core):
    half = v.shape[0] // 2
    return (
        lax.dynamic_slice_in_dim(v, core * half, half, 0),
        lax.dynamic_slice_in_dim(v, (1 - core) * half, half, 0),
    )


def low(v):
    return v.astype(jnp.bfloat16)


def wide(v):
    return v.astype(jnp.float32)


def local(x):
    core = lax.axis_index("core")

    def pair_sum(blocks):
        mine, other = blocks
        got = swap(low(dot(x, other, ((1,), (1,)))), "core")
        pair = low(dot(x, mine, ((1,), (1,))) + wide(got))
        return pair.reshape(8, pair.shape[0] // 8, pair.shape[1])

    def exchange_z(pair):
        return lax.all_to_all(pair, "z", 0, 0)

    def finish(split):
        plane = low(jnp.sum(wide(split), axis=0))
        return low(wide(plane) + wide(swap(plane, "x_hi")))

    parts, sent = gather_tp(*halves(x, core), (pair_sum, exchange_z))
    rows = [finish(sent), finish(exchange_z(pair_sum(parts[1])))]
    rows = jnp.concatenate(rows, axis=1)
    gram_mine = gather_z(rows, jnp.zeros((8 * rows.shape[0], rows.shape[1]), rows.dtype))
    gram_other = swap(gram_mine, "core")
    n = rows.shape[1] // 2
    grams = [(gram_mine[:, :n], gram_other[:, :n]), (gram_mine[:, n:], gram_other[:, n:])]

    def apply(blocks):
        total = 0
        for gram, block in zip(grams, blocks):
            for g, b in zip(gram, block):
                total = total + dot(g, b, ((1,), (0,)))
        return total

    applied = apply(parts)
    twice_applied = apply(gather_tp(*halves(low(applied), core)))
    mixed = (
        quintic_one * x.astype(jnp.float32)
        + quintic_three * applied
        + quintic_five * twice_applied
    )
    return mixed * math.sqrt(C)


def solution(mesh):
    grid = Mesh(mesh.devices.reshape(8, 2, 2, 2, 4), ("z", "x_hi", "core", "x_lo", "y"))
    spec = P(TP, ("z", "x_hi", "core"))
    return jax.shard_map(local, mesh=grid, in_specs=(spec,), out_specs=spec, check_vma=False)
```

```python
import math

import jax
import jax.numpy as jnp
from jax import lax
from jax.sharding import Mesh, PartitionSpec as P

C = 18432


quintic_one = 3.4445
quintic_three = -4.775
quintic_five = 2.0315

TP = ("x_lo", "y")
SWAP = [(0, 1), (1, 0)]


def dot(a, b, dims):
    return lax.dot_general(a, b, (dims, ((), ())), preferred_element_type=jnp.float32)


def shift(v, axis, size, by):
    return lax.ppermute(v, axis, [(i, (i + by) % size) for i in range(size)])


def swap(v, axis):
    return lax.ppermute(v, axis, SWAP)


def gather_tp(first, second, early_work=None):
    h = second.shape[0] // 2
    wave = (
        swap(first, "x_lo"),
        shift(first, "y", 4, 1),
        shift(first, "y", 4, -1),
        swap(second, "x_lo"),
        shift(second, "y", 4, 1),
        shift(second, "y", 4, -1),
    )
    f_x, f_left, f_right, s_x, s_left, s_right = lax.optimization_barrier(wave)
    early = (
        jnp.concatenate([first, f_x, f_left, f_right], axis=0),
        jnp.concatenate([second, s_x, s_left, s_right], axis=0),
    )
    wave = (
        shift(f_x, "y", 4, 1),
        shift(f_x, "y", 4, -1),
        swap(s_left, "x_lo"),
        swap(s_right, "x_lo"),
        shift(s_left[:h], "y", 4, 1),
        shift(s_right[h:], "y", 4, -1),
    )
    done = early_work(early) if early_work is not None else early
    (fx_left, fx_right, sx_left, sx_right, far_low, far_high), done = lax.optimization_barrier((wave, done))
    s_far = jnp.concatenate([far_low, far_high], axis=0)
    f_far = shift(f_left, "y", 4, 1)
    fx_far = shift(fx_right, "y", 4, -1)
    sx_far = swap(s_far, "x_lo")
    late = (
        jnp.concatenate([fx_left, fx_right, f_far, fx_far], axis=0),
        jnp.concatenate([sx_left, sx_right, s_far, sx_far], axis=0),
    )
    return early, late, done


def gather_z(v, base):
    rows, columns = v.shape
    h = columns // 2
    z = lax.axis_index("z")
    r1 = shift(v, "z", 8, 1)
    l1 = shift(v, "z", 8, -1)
    r2 = shift(v, "z", 8, 2)
    l2 = shift(v, "z", 8, -2)
    r3 = shift(r1, "z", 8, 2)
    l3 = shift(l1, "z", 8, -2)
    far = jnp.concatenate([shift(r3[:, :h], "z", 8, 1), shift(l3[:, h:], "z", 8, -1)], axis=1)
    out = base
    for by, piece in ((0, v), (-1, r1), (1, l1), (-2, r2), (2, l2), (-3, r3), (3, l3), (4, far)):
        out = lax.dynamic_update_slice_in_dim(out, piece, lax.rem(z + by + 8, 8) * rows, 0)
    return out


def halves(v, core):
    half = v.shape[0] // 2
    return (
        lax.dynamic_slice_in_dim(v, core * half, half, 0),
        lax.dynamic_slice_in_dim(v, (1 - core) * half, half, 0),
    )


def low(v):
    return v.astype(jnp.bfloat16)


def wide(v):
    return v.astype(jnp.float32)


def local(x):
    core = lax.axis_index("core")

    def pair_sum(blocks):
        mine, other = blocks
        got = swap(low(dot(x, other, ((1,), (1,)))), "core")
        pair = low(dot(x, mine, ((1,), (1,))) + wide(got))
        return pair.reshape(8, pair.shape[0] // 8, pair.shape[1])

    def exchange_z(pair):
        return lax.all_to_all(pair, "z", 0, 0)

    def finish(split):
        plane = low(jnp.sum(wide(split), axis=0))
        return low(wide(plane) + wide(swap(plane, "x_hi")))

    *parts, pair = gather_tp(*halves(x, core), pair_sum)
    sent = exchange_z(pair)
    sent, pair = lax.optimization_barrier((sent, pair_sum(parts[1])))
    rows = [finish(sent), finish(exchange_z(pair))]
    rows = jnp.concatenate(rows, axis=1)
    gram_mine = gather_z(rows, jnp.zeros((8 * rows.shape[0], rows.shape[1]), rows.dtype))
    gram_other = swap(gram_mine, "core")
    n = rows.shape[1] // 2
    grams = [(gram_mine[:, :n], gram_other[:, :n]), (gram_mine[:, n:], gram_other[:, n:])]

    def apply(blocks):
        total = 0
        for gram, block in zip(grams, blocks):
            for g, b in zip(gram, block):
                total = total + dot(g, b, ((1,), (0,)))
        return total

    applied = apply(parts)
    twice_applied = apply(gather_tp(*halves(low(applied), core))[:2])
    mixed = (
        quintic_one * x.astype(jnp.float32)
        + quintic_three * applied
        + quintic_five * twice_applied
    )
    return mixed * math.sqrt(C)


def solution(mesh):
    grid = Mesh(mesh.devices.reshape(8, 2, 2, 2, 4), ("z", "x_hi", "core", "x_lo", "y"))
    spec = P(TP, ("z", "x_hi", "core"))
    return jax.shard_map(local, mesh=grid, in_specs=(spec,), out_specs=spec, check_vma=False)
```

```python
import math

import jax
import jax.numpy as jnp
from jax import lax
from jax.sharding import Mesh, PartitionSpec as P

C = 18432


quintic_one = 3.4445
quintic_three = -4.775
quintic_five = 2.0315

TP = ("x_lo", "y")
SWAP = [(0, 1), (1, 0)]


def dot(a, b, dims):
    return lax.dot_general(a, b, (dims, ((), ())), preferred_element_type=jnp.float32)


def shift(v, axis, size, by):
    return lax.ppermute(v, axis, [(i, (i + by) % size) for i in range(size)])


def swap(v, axis):
    return lax.ppermute(v, axis, SWAP)


def gather_tp(mine, other):
    cut = mine.shape[0] // 7 * 4
    h = mine.shape[0] - cut
    first = jnp.concatenate([mine[:cut], other[:cut]], axis=0)
    second = jnp.concatenate([mine[cut:], other[cut:]], axis=0)
    s_left = shift(second, "y", 4, 1)
    s_right = shift(second, "y", 4, -1)
    f_x = swap(first, "x_lo")
    s_x = swap(second, "x_lo")
    f_left = shift(first, "y", 4, 1)
    f_right = shift(first, "y", 4, -1)
    far_low = shift(s_left[:h], "y", 4, 1)
    far_high = shift(s_right[h:], "y", 4, -1)
    fx_left = shift(f_x, "y", 4, 1)
    fx_right = shift(f_x, "y", 4, -1)
    sx_left = swap(s_left, "x_lo")
    sx_right = swap(s_right, "x_lo")
    f_far = shift(f_left, "y", 4, 1)
    fx_far = shift(fx_right, "y", 4, -1)
    sx_far_low = swap(far_low, "x_lo")
    sx_far_high = swap(far_high, "x_lo")
    return (
        [first, f_x, f_left, f_right, fx_left, fx_right, f_far, fx_far],
        [second, s_x, s_left, s_right, sx_left, sx_right],
        [(far_low, far_high), (sx_far_low, sx_far_high)],
    )


def stacks(firsts, seconds, fars):
    cut = firsts[0].shape[0] // 2
    h = seconds[0].shape[0] // 2
    mine = [v[:cut] for v in firsts] + [v[:h] for v in seconds] + [v[0] for v in fars]
    other = [v[cut:] for v in firsts] + [v[h:] for v in seconds] + [v[1] for v in fars]
    return jnp.concatenate(mine, axis=0), jnp.concatenate(other, axis=0)


def gather_z(v, base):
    rows, columns = v.shape
    h = columns // 2
    z = lax.axis_index("z")
    r1 = shift(v, "z", 8, 1)
    l1 = shift(v, "z", 8, -1)
    r2 = shift(v, "z", 8, 2)
    l2 = shift(v, "z", 8, -2)
    r3 = shift(r1, "z", 8, 2)
    l3 = shift(l1, "z", 8, -2)
    far = jnp.concatenate([shift(r3[:, :h], "z", 8, 1), shift(l3[:, h:], "z", 8, -1)], axis=1)
    out = base
    for by, piece in ((0, v), (-1, r1), (1, l1), (-2, r2), (2, l2), (-3, r3), (3, l3), (4, far)):
        out = lax.dynamic_update_slice_in_dim(out, piece, lax.rem(z + by + 8, 8) * rows, 0)
    return out


def halves(v, core):
    half = v.shape[0] // 2
    return (
        lax.dynamic_slice_in_dim(v, core * half, half, 0),
        lax.dynamic_slice_in_dim(v, (1 - core) * half, half, 0),
    )


def low(v):
    return v.astype(jnp.bfloat16)


def wide(v):
    return v.astype(jnp.float32)


def local(x):
    core = lax.axis_index("core")

    def pair_sum(blocks):
        mine, other = blocks
        got = swap(low(dot(x, other, ((1,), (1,)))), "core")
        pair = low(dot(x, mine, ((1,), (1,))) + wide(got))
        return pair.reshape(8, pair.shape[0] // 8, pair.shape[1])

    def exchange_z(pair):
        return lax.all_to_all(pair, "z", 0, 0)

    def finish(split):
        plane = low(jnp.sum(wide(split), axis=0))
        return low(wide(plane) + wide(swap(plane, "x_hi")))

    blocks = stacks(*lax.optimization_barrier(gather_tp(*halves(x, core))))
    rows = finish(exchange_z(pair_sum(blocks)))
    gram_mine = gather_z(rows, jnp.zeros((8 * rows.shape[0], rows.shape[1]), rows.dtype))
    gram_other = swap(gram_mine, "core")

    def apply(blocks):
        mine, other = blocks
        return dot(gram_mine, mine, ((1,), (0,))) + dot(gram_other, other, ((1,), (0,)))

    applied = apply(blocks)
    twice_applied = apply(stacks(*gather_tp(*halves(low(applied), core))))
    mixed = (
        quintic_one * x.astype(jnp.float32)
        + quintic_three * applied
        + quintic_five * twice_applied
    )
    return mixed * math.sqrt(C)


def solution(mesh):
    grid = Mesh(mesh.devices.reshape(8, 2, 2, 2, 4), ("z", "x_hi", "core", "x_lo", "y"))
    spec = P(TP, ("z", "x_hi", "core"))
    return jax.shard_map(local, mesh=grid, in_specs=(spec,), out_specs=spec, check_vma=False)
```

```python
import math

import jax
import jax.numpy as jnp
from jax import lax
from jax.sharding import Mesh, PartitionSpec as P

C = 18432


quintic_one = 3.4445
quintic_three = -4.775
quintic_five = 2.0315

TP = ("x_lo", "y")
SWAP = [(0, 1), (1, 0)]


def dot(a, b, dims):
    return lax.dot_general(a, b, (dims, ((), ())), preferred_element_type=jnp.float32)


def shift(v, axis, size, by):
    return lax.ppermute(v, axis, [(i, (i + by) % size) for i in range(size)])


def swap(v, axis):
    return lax.ppermute(v, axis, SWAP)


def gather_tp(first, second, early_work=None):
    h = second.shape[0] // 2
    wave = (
        swap(first, "x_lo"),
        shift(first, "y", 4, 1),
        shift(first, "y", 4, -1),
        swap(second, "x_lo"),
        shift(second, "y", 4, 1),
        shift(second, "y", 4, -1),
    )
    f_x, f_left, f_right, s_x, s_left, s_right = lax.optimization_barrier(wave)
    early = (
        jnp.concatenate([first, f_x, f_left, f_right], axis=0),
        jnp.concatenate([second, s_x, s_left, s_right], axis=0),
    )
    wave = (
        shift(f_x, "y", 4, 1),
        shift(f_x, "y", 4, -1),
        swap(s_left, "x_lo"),
        shift(s_left[:h], "y", 4, 1),
        shift(s_right[h:], "y", 4, -1),
    )
    done = early_work(early) if early_work is not None else early
    (fx_left, fx_right, sx_left, far_low, far_high), done = lax.optimization_barrier((wave, done))
    sx_right = swap(s_right, "x_lo")
    s_far = jnp.concatenate([far_low, far_high], axis=0)
    f_far = shift(f_left, "y", 4, 1)
    fx_far = shift(fx_right, "y", 4, -1)
    sx_far = swap(s_far, "x_lo")
    late = (
        jnp.concatenate([fx_left, fx_right, f_far, fx_far], axis=0),
        jnp.concatenate([sx_left, sx_right, s_far, sx_far], axis=0),
    )
    return early, late, done


def gather_z(v, base):
    rows, columns = v.shape
    h = columns // 2
    z = lax.axis_index("z")
    r1 = shift(v, "z", 8, 1)
    l1 = shift(v, "z", 8, -1)
    r3 = shift(r1, "z", 8, 2)
    l3 = shift(l1, "z", 8, -2)
    r2 = shift(r1, "z", 8, 1)
    l2 = shift(l1, "z", 8, -1)
    far = jnp.concatenate([shift(r3[:, :h], "z", 8, 1), shift(l3[:, h:], "z", 8, -1)], axis=1)
    out = base
    for by, piece in ((0, v), (-1, r1), (1, l1), (-2, r2), (2, l2), (-3, r3), (3, l3), (4, far)):
        out = lax.dynamic_update_slice_in_dim(out, piece, lax.rem(z + by + 8, 8) * rows, 0)
    return out


def halves(v, core):
    half = v.shape[0] // 2
    return (
        lax.dynamic_slice_in_dim(v, core * half, half, 0),
        lax.dynamic_slice_in_dim(v, (1 - core) * half, half, 0),
    )


def low(v):
    return v.astype(jnp.bfloat16)


def wide(v):
    return v.astype(jnp.float32)


def local(x):
    core = lax.axis_index("core")

    def pair_sum(blocks):
        mine, other = blocks
        got = swap(low(dot(x, other, ((1,), (1,)))), "core")
        pair = low(dot(x, mine, ((1,), (1,))) + wide(got))
        return pair.reshape(8, pair.shape[0] // 8, pair.shape[1])

    def exchange_z(pair):
        return lax.all_to_all(pair, "z", 0, 0)

    def finish(split):
        plane = low(jnp.sum(wide(split), axis=0))
        return low(wide(plane) + wide(swap(plane, "x_hi")))

    *parts, pair = gather_tp(*halves(x, core), pair_sum)
    sent = exchange_z(pair)
    sent, pair = lax.optimization_barrier((sent, pair_sum(parts[1])))
    rows = [finish(sent), finish(exchange_z(pair))]
    rows = jnp.concatenate(rows, axis=1)
    gram_mine = gather_z(rows, jnp.zeros((8 * rows.shape[0], rows.shape[1]), rows.dtype))
    gram_other = swap(gram_mine, "core")
    n = rows.shape[1] // 2
    grams = [(gram_mine[:, :n], gram_other[:, :n]), (gram_mine[:, n:], gram_other[:, n:])]

    def apply(blocks):
        total = 0
        for gram, block in zip(grams, blocks):
            for g, b in zip(gram, block):
                total = total + dot(g, b, ((1,), (0,)))
        return total

    applied = apply(parts)
    twice_applied = apply(gather_tp(*halves(low(applied), core))[:2])
    mixed = (
        quintic_one * x.astype(jnp.float32)
        + quintic_three * applied
        + quintic_five * twice_applied
    )
    return mixed * math.sqrt(C)


def solution(mesh):
    grid = Mesh(mesh.devices.reshape(8, 2, 2, 2, 4), ("z", "x_hi", "core", "x_lo", "y"))
    spec = P(TP, ("z", "x_hi", "core"))
    return jax.shard_map(local, mesh=grid, in_specs=(spec,), out_specs=spec, check_vma=False)
```

```python
import math

import jax
import jax.numpy as jnp
from jax import lax
from jax.sharding import Mesh, PartitionSpec as P

C = 18432


quintic_one = 3.4445
quintic_three = -4.775
quintic_five = 2.0315

TP = ("x_lo", "y")
SWAP = [(0, 1), (1, 0)]


def dot(a, b, dims):
    return lax.dot_general(a, b, (dims, ((), ())), preferred_element_type=jnp.float32)


def shift(v, axis, size, by):
    return lax.ppermute(v, axis, [(i, (i + by) % size) for i in range(size)])


def swap(v, axis):
    return lax.ppermute(v, axis, SWAP)


def gather_tp(first, second, early_work=None):
    n = first.shape[0]
    h = n // 2
    whole = jnp.concatenate([first, second], axis=0)
    wave = (swap(whole, "x_lo"), shift(whole, "y", 4, 1), shift(whole, "y", 4, -1))
    (f_x, s_x), (f_left, s_left), (f_right, s_right) = (
        (v[:n], v[n:]) for v in lax.optimization_barrier(wave)
    )
    early = (
        jnp.concatenate([first, f_x, f_left, f_right], axis=0),
        jnp.concatenate([second, s_x, s_left, s_right], axis=0),
    )
    wave = (
        shift(jnp.concatenate([f_x, s_left[:h]], axis=0), "y", 4, 1),
        shift(jnp.concatenate([f_x, s_right[h:]], axis=0), "y", 4, -1),
        swap(s_left, "x_lo"),
    )
    done = early_work(early) if early_work is not None else early
    (to_right, to_left, sx_left), done = lax.optimization_barrier((wave, done))
    fx_left, far_low = to_right[:n], to_right[n:]
    fx_right, far_high = to_left[:n], to_left[n:]
    sx_right = swap(s_right, "x_lo")
    s_far = jnp.concatenate([far_low, far_high], axis=0)
    f_far = shift(f_left, "y", 4, 1)
    fx_far = shift(fx_right, "y", 4, -1)
    sx_far = swap(s_far, "x_lo")
    late = (
        jnp.concatenate([fx_left, fx_right, f_far, fx_far], axis=0),
        jnp.concatenate([sx_left, sx_right, s_far, sx_far], axis=0),
    )
    return early, late, done


def gather_z(v, base):
    rows, columns = v.shape
    h = columns // 2
    z = lax.axis_index("z")
    r1 = shift(v, "z", 8, 1)
    l1 = shift(v, "z", 8, -1)
    r2 = shift(r1, "z", 8, 1)
    l2 = shift(l1, "z", 8, -1)
    r3 = shift(r1, "z", 8, 2)
    l3 = shift(l1, "z", 8, -2)
    far = jnp.concatenate([shift(r2[:, :h], "z", 8, 2), shift(l2[:, h:], "z", 8, -2)], axis=1)
    out = base
    for by, piece in ((0, v), (-1, r1), (1, l1), (-2, r2), (2, l2), (-3, r3), (3, l3), (4, far)):
        out = lax.dynamic_update_slice_in_dim(out, piece, lax.rem(z + by + 8, 8) * rows, 0)
    return out


def halves(v, core):
    half = v.shape[0] // 2
    return (
        lax.dynamic_slice_in_dim(v, core * half, half, 0),
        lax.dynamic_slice_in_dim(v, (1 - core) * half, half, 0),
    )


def low(v):
    return v.astype(jnp.bfloat16)


def wide(v):
    return v.astype(jnp.float32)


def local(x):
    core = lax.axis_index("core")

    def pair_sum(blocks):
        mine, other = blocks
        got = swap(low(dot(x, other, ((1,), (1,)))), "core")
        pair = low(dot(x, mine, ((1,), (1,))) + wide(got))
        return pair.reshape(8, pair.shape[0] // 8, pair.shape[1])

    def exchange_z(pair):
        return lax.all_to_all(pair, "z", 0, 0)

    def finish(split):
        plane = low(jnp.sum(wide(split), axis=0))
        return low(wide(plane) + wide(swap(plane, "x_hi")))

    *parts, pair = gather_tp(*halves(x, core), pair_sum)
    sent = exchange_z(pair)
    sent, pair = lax.optimization_barrier((sent, pair_sum(parts[1])))
    rows = [finish(sent), finish(exchange_z(pair))]
    rows = jnp.concatenate(rows, axis=1)
    gram_mine = gather_z(rows, jnp.zeros((8 * rows.shape[0], rows.shape[1]), rows.dtype))
    gram_other = swap(gram_mine, "core")
    n = rows.shape[1] // 2
    grams = [(gram_mine[:, :n], gram_other[:, :n]), (gram_mine[:, n:], gram_other[:, n:])]

    def apply(blocks):
        total = 0
        for gram, block in zip(grams, blocks):
            for g, b in zip(gram, block):
                total = total + dot(g, b, ((1,), (0,)))
        return total

    applied = apply(parts)
    twice_applied = apply(gather_tp(*halves(low(applied), core))[:2])
    mixed = (
        quintic_one * x.astype(jnp.float32)
        + quintic_three * applied
        + quintic_five * twice_applied
    )
    return mixed * math.sqrt(C)


def solution(mesh):
    grid = Mesh(mesh.devices.reshape(8, 2, 2, 2, 4), ("z", "x_hi", "core", "x_lo", "y"))
    spec = P(TP, ("z", "x_hi", "core"))
    return jax.shard_map(local, mesh=grid, in_specs=(spec,), out_specs=spec, check_vma=False)
```

```python
import math

import jax
import jax.numpy as jnp
from jax import lax
from jax.sharding import Mesh, PartitionSpec as P

C = 18432


quintic_one = 3.4445
quintic_three = -4.775
quintic_five = 2.0315

TP = ("x_lo", "y")
SWAP = [(0, 1), (1, 0)]


def dot(a, b, dims):
    return lax.dot_general(a, b, (dims, ((), ())), preferred_element_type=jnp.float32)


def shift(v, axis, size, by):
    return lax.ppermute(v, axis, [(i, (i + by) % size) for i in range(size)])


def swap(v, axis):
    return lax.ppermute(v, axis, SWAP)


def gather_tp(first, second, early_work=None):
    n = first.shape[0]
    h = n // 2
    whole = jnp.concatenate([first, second], axis=0)
    wave = (swap(whole, "x_lo"), shift(whole, "y", 4, 1), shift(whole, "y", 4, -1))
    (f_x, s_x), (f_left, s_left), (f_right, s_right) = (
        (v[:n], v[n:]) for v in lax.optimization_barrier(wave)
    )
    early = (
        jnp.concatenate([first, f_x, f_left, f_right], axis=0),
        jnp.concatenate([second, s_x, s_left, s_right], axis=0),
    )
    right = jnp.concatenate([f_x, s_left[:h]], axis=0)
    left = jnp.concatenate([f_x, s_right[h:]], axis=0)
    across = s_left if early_work is not None else jnp.concatenate([s_left, s_right], axis=0)
    wave = (shift(right, "y", 4, 1), shift(left, "y", 4, -1), swap(across, "x_lo"))
    done = early_work(early) if early_work is not None else early
    (to_right, to_left, across), done = lax.optimization_barrier((wave, done))
    fx_left, far_low = to_right[:n], to_right[n:]
    fx_right, far_high = to_left[:n], to_left[n:]
    far = [far_low, far_high]
    if early_work is not None:
        last = swap(jnp.concatenate([s_right] + far, axis=0), "x_lo")
    else:
        last = swap(jnp.concatenate(far, axis=0), "x_lo")
    wave = (last, shift(f_left, "y", 4, 1), shift(fx_right, "y", 4, -1))
    last, f_far, fx_far = lax.optimization_barrier(wave)
    s_late = [across, far_low, far_high, last]
    if early_work is not None:
        s_late = [across, last[:n], far_low, far_high, last[n:]]
    late = (
        jnp.concatenate([fx_left, fx_right, f_far, fx_far], axis=0),
        jnp.concatenate(s_late, axis=0),
    )
    return early, late, done


def gather_z(v, base):
    rows, columns = v.shape
    h = columns // 2
    z = lax.axis_index("z")
    r1 = shift(v, "z", 8, 1)
    l1 = shift(v, "z", 8, -1)
    r2 = shift(r1, "z", 8, 1)
    l2 = shift(l1, "z", 8, -1)
    r3 = shift(r1, "z", 8, 2)
    l3 = shift(l1, "z", 8, -2)
    far = jnp.concatenate([shift(r2[:, :h], "z", 8, 2), shift(l2[:, h:], "z", 8, -2)], axis=1)
    out = base
    for by, piece in ((0, v), (-1, r1), (1, l1), (-2, r2), (2, l2), (-3, r3), (3, l3), (4, far)):
        out = lax.dynamic_update_slice_in_dim(out, piece, lax.rem(z + by + 8, 8) * rows, 0)
    return out


def halves(v, core):
    half = v.shape[0] // 2
    return (
        lax.dynamic_slice_in_dim(v, core * half, half, 0),
        lax.dynamic_slice_in_dim(v, (1 - core) * half, half, 0),
    )


def low(v):
    return v.astype(jnp.bfloat16)


def wide(v):
    return v.astype(jnp.float32)


def local(x):
    core = lax.axis_index("core")

    def pair_sum(blocks):
        mine, other = blocks
        got = swap(low(dot(x, other, ((1,), (1,)))), "core")
        pair = low(dot(x, mine, ((1,), (1,))) + wide(got))
        return pair.reshape(8, pair.shape[0] // 8, pair.shape[1])

    def exchange_z(pair):
        return lax.all_to_all(pair, "z", 0, 0)

    def finish(split):
        plane = low(jnp.sum(wide(split), axis=0))
        return low(wide(plane) + wide(swap(plane, "x_hi")))

    *parts, pair = gather_tp(*halves(x, core), pair_sum)
    sent = exchange_z(pair)
    sent, pair = lax.optimization_barrier((sent, pair_sum(parts[1])))
    rows = [finish(sent), finish(exchange_z(pair))]
    rows = jnp.concatenate(rows, axis=1)
    gram_mine = gather_z(rows, jnp.zeros((8 * rows.shape[0], rows.shape[1]), rows.dtype))
    gram_other = swap(gram_mine, "core")
    n = rows.shape[1] // 2
    grams = [g[:, i : i + n] for i in (0, n) for g in (gram_mine, gram_other)]

    def apply(blocks, order):
        flat = [b for part in blocks for b in part]
        total = 0
        for i in order:
            total = total + dot(grams[i], flat[i], ((1,), (0,)))
        return total

    applied = apply(parts, (0, 2, 1, 3))
    twice_applied = apply(gather_tp(*halves(low(applied), core))[:2], (0, 1, 2, 3))
    mixed = (
        quintic_one * x.astype(jnp.float32)
        + quintic_three * applied
        + quintic_five * twice_applied
    )
    return mixed * math.sqrt(C)


def solution(mesh):
    grid = Mesh(mesh.devices.reshape(8, 2, 2, 2, 4), ("z", "x_hi", "core", "x_lo", "y"))
    spec = P(TP, ("z", "x_hi", "core"))
    return jax.shard_map(local, mesh=grid, in_specs=(spec,), out_specs=spec, check_vma=False)
```

```python
import math

import jax
import jax.numpy as jnp
from jax import lax
from jax.sharding import Mesh, PartitionSpec as P

C = 18432


quintic_one = 3.4445
quintic_three = -4.775
quintic_five = 2.0315

TP = ("x_lo", "y")
SWAP = [(0, 1), (1, 0)]


def dot(a, b, dims):
    return lax.dot_general(a, b, (dims, ((), ())), preferred_element_type=jnp.float32)


def shift(v, axis, size, by):
    return lax.ppermute(v, axis, [(i, (i + by) % size) for i in range(size)])


def swap(v, axis):
    return lax.ppermute(v, axis, SWAP)


def gather_tp(first, second, early_work=None):
    n = first.shape[0]
    h = n // 2
    whole = jnp.concatenate([first, second], axis=0)
    wave = (swap(whole, "x_lo"), shift(whole, "y", 4, 1), shift(whole, "y", 4, -1))
    (f_x, s_x), (f_left, s_left), (f_right, s_right) = (
        (v[:n], v[n:]) for v in lax.optimization_barrier(wave)
    )
    early = (
        jnp.concatenate([first, f_x, f_left, f_right], axis=0),
        jnp.concatenate([second, s_x, s_left, s_right], axis=0),
    )
    right = jnp.concatenate([f_x, s_left[:h]], axis=0)
    left = jnp.concatenate([f_x, s_right[h:]], axis=0)
    h_right = shift(right, "y", 4, 1)
    h_left = shift(left, "y", 4, -1)
    if early_work is not None:
        wave = (h_right, h_left, swap(s_left, "x_lo"))
        (h_right, h_left, sx_left), done = lax.optimization_barrier((wave, early_work(early)))
        far = [h_right[n:], h_left[n:]]
        last = swap(jnp.concatenate([s_right] + far, axis=0), "x_lo")
        s_late = [sx_left, last[:n]] + far + [last[n:]]
    else:
        done = early
        across = swap(jnp.concatenate([s_left, s_right], axis=0), "x_lo")
        far = [h_right[n:], h_left[n:]]
        s_late = [across] + far + [swap(jnp.concatenate(far, axis=0), "x_lo")]
    fx_left, fx_right = h_right[:n], h_left[:n]
    f_far = shift(f_left, "y", 4, 1)
    fx_far = shift(fx_right, "y", 4, -1)
    late = (
        jnp.concatenate([fx_left, fx_right, f_far, fx_far], axis=0),
        jnp.concatenate(s_late, axis=0),
    )
    return early, late, done


def gather_z(v, base):
    rows, columns = v.shape
    h = columns // 2
    z = lax.axis_index("z")
    r1 = shift(v, "z", 8, 1)
    l1 = shift(v, "z", 8, -1)
    r2 = shift(r1, "z", 8, 1)
    l2 = shift(l1, "z", 8, -1)
    r3 = shift(r1, "z", 8, 2)
    l3 = shift(l1, "z", 8, -2)
    far = jnp.concatenate([shift(r2[:, :h], "z", 8, 2), shift(l2[:, h:], "z", 8, -2)], axis=1)
    out = base
    for by, piece in ((0, v), (-1, r1), (1, l1), (-2, r2), (2, l2), (-3, r3), (3, l3), (4, far)):
        out = lax.dynamic_update_slice_in_dim(out, piece, lax.rem(z + by + 8, 8) * rows, 0)
    return out


def halves(v, core):
    half = v.shape[0] // 2
    return (
        lax.dynamic_slice_in_dim(v, core * half, half, 0),
        lax.dynamic_slice_in_dim(v, (1 - core) * half, half, 0),
    )


def low(v):
    return v.astype(jnp.bfloat16)


def wide(v):
    return v.astype(jnp.float32)


def local(x):
    core = lax.axis_index("core")

    def pair_sum(blocks):
        mine, other = blocks
        got = swap(low(dot(x, other, ((1,), (1,)))), "core")
        pair = low(dot(x, mine, ((1,), (1,))) + wide(got))
        return pair.reshape(8, pair.shape[0] // 8, pair.shape[1])

    def exchange_z(pair):
        return lax.all_to_all(pair, "z", 0, 0)

    def finish(split):
        plane = low(jnp.sum(wide(split), axis=0))
        return low(wide(plane) + wide(swap(plane, "x_hi")))

    *parts, pair = gather_tp(*halves(x, core), pair_sum)
    sent = exchange_z(pair)
    sent, pair = lax.optimization_barrier((sent, pair_sum(parts[1])))
    rows = [finish(sent), finish(exchange_z(pair))]
    rows = jnp.concatenate(rows, axis=1)
    gram_mine = gather_z(rows, jnp.zeros((8 * rows.shape[0], rows.shape[1]), rows.dtype))
    gram_other = swap(gram_mine, "core")
    n = rows.shape[1] // 2
    grams = [g[:, i : i + n] for i in (0, n) for g in (gram_mine, gram_other)]

    def apply(blocks, order):
        flat = [b for part in blocks for b in part]
        total = 0
        for i in order:
            total = total + dot(grams[i], flat[i], ((1,), (0,)))
        return total

    applied = apply(parts, (0, 2, 1, 3))
    twice_applied = apply(gather_tp(*halves(low(applied), core))[:2], (0, 1, 2, 3))
    mixed = (
        quintic_one * x.astype(jnp.float32)
        + quintic_three * applied
        + quintic_five * twice_applied
    )
    return mixed * math.sqrt(C)


def solution(mesh):
    grid = Mesh(mesh.devices.reshape(8, 2, 2, 2, 4), ("z", "x_hi", "core", "x_lo", "y"))
    spec = P(TP, ("z", "x_hi", "core"))
    return jax.shard_map(local, mesh=grid, in_specs=(spec,), out_specs=spec, check_vma=False)
```

```python
import math

import jax
import jax.numpy as jnp
from jax import lax
from jax.sharding import Mesh, PartitionSpec as P

C = 18432


quintic_one = 3.4445
quintic_three = -4.775
quintic_five = 2.0315

TP = ("x_lo", "y")
SWAP = [(0, 1), (1, 0)]


def dot(a, b, dims):
    return lax.dot_general(a, b, (dims, ((), ())), preferred_element_type=jnp.float32)


def shift(v, axis, size, by):
    return lax.ppermute(v, axis, [(i, (i + by) % size) for i in range(size)])


def swap(v, axis):
    return lax.ppermute(v, axis, SWAP)


def gather_tp(first, second, early_work=None):
    n = first.shape[0]
    h = n // 2
    whole = jnp.concatenate([first, second], axis=0)
    wave = (swap(whole, "x_lo"), shift(whole, "y", 4, 1), shift(whole, "y", 4, -1))
    (f_x, s_x), (f_left, s_left), (f_right, s_right) = (
        (v[:n], v[n:]) for v in lax.optimization_barrier(wave)
    )
    early = (
        jnp.concatenate([first, f_x, f_left, f_right], axis=0),
        jnp.concatenate([second, s_x, s_left, s_right], axis=0),
    )
    wave = (
        shift(jnp.concatenate([f_x, s_left[:h]], axis=0), "y", 4, 1),
        shift(jnp.concatenate([f_x, s_right[h:]], axis=0), "y", 4, -1),
        swap(s_left, "x_lo"),
    )
    done = early_work(early) if early_work is not None else early
    (to_right, to_left, sx_left), done = lax.optimization_barrier((wave, done))
    fx_left, far_low = to_right[:n], to_right[n:]
    fx_right, far_high = to_left[:n], to_left[n:]
    sx_right = swap(s_right, "x_lo")
    s_far = jnp.concatenate([far_low, far_high], axis=0)
    f_far = shift(f_left, "y", 4, 1)
    fx_far = shift(fx_right, "y", 4, -1)
    sx_far = swap(s_far, "x_lo")
    late = (
        jnp.concatenate([fx_left, f_far, fx_right, fx_far], axis=0),
        jnp.concatenate([sx_left, s_far, sx_right, sx_far], axis=0),
    )
    return early, late, done


def gather_z(v, base):
    rows, columns = v.shape
    h = columns // 2
    z = lax.axis_index("z")
    r1 = shift(v, "z", 8, 1)
    l1 = shift(v, "z", 8, -1)
    r2 = shift(r1, "z", 8, 1)
    l2 = shift(l1, "z", 8, -1)
    r3 = shift(r1, "z", 8, 2)
    l3 = shift(l1, "z", 8, -2)
    far = jnp.concatenate([shift(r2[:, :h], "z", 8, 2), shift(l2[:, h:], "z", 8, -2)], axis=1)
    out = base
    for by, piece in ((0, v), (-1, r1), (1, l1), (-2, r2), (2, l2), (-3, r3), (3, l3), (4, far)):
        out = lax.dynamic_update_slice_in_dim(out, piece, lax.rem(z + by + 8, 8) * rows, 0)
    return out


def halves(v, core):
    half = v.shape[0] // 2
    return (
        lax.dynamic_slice_in_dim(v, core * half, half, 0),
        lax.dynamic_slice_in_dim(v, (1 - core) * half, half, 0),
    )


def low(v):
    return v.astype(jnp.bfloat16)


def wide(v):
    return v.astype(jnp.float32)


def local(x):
    core = lax.axis_index("core")

    def pair_sum(blocks):
        mine, other = blocks
        got = swap(low(dot(x, other, ((1,), (1,)))), "core")
        pair = low(dot(x, mine, ((1,), (1,))) + wide(got))
        return pair.reshape(8, pair.shape[0] // 8, pair.shape[1])

    def exchange_z(pair):
        return lax.all_to_all(pair, "z", 0, 0)

    def finish(split):
        plane = low(jnp.sum(wide(split), axis=0))
        return low(wide(plane) + wide(swap(plane, "x_hi")))

    *parts, pair = gather_tp(*halves(x, core), pair_sum)
    sent = exchange_z(pair)
    sent, pair = lax.optimization_barrier((sent, pair_sum(parts[1])))
    rows = [finish(sent), finish(exchange_z(pair))]
    rows = jnp.concatenate(rows, axis=1)
    gram_mine = gather_z(rows, jnp.zeros((8 * rows.shape[0], rows.shape[1]), rows.dtype))
    gram_other = swap(gram_mine, "core")
    n = rows.shape[1] // 2
    grams = [g[:, i : i + n] for i in (0, n) for g in (gram_mine, gram_other)]

    def apply(blocks, order):
        flat = [b for part in blocks for b in part]
        total = 0
        for i in order:
            total = total + dot(grams[i], flat[i], ((1,), (0,)))
        return total

    applied = apply(parts, (0, 2, 1, 3))
    twice_applied = apply(gather_tp(*halves(low(applied), core))[:2], (0, 1, 2, 3))
    mixed = (
        quintic_one * x.astype(jnp.float32)
        + quintic_three * applied
        + quintic_five * twice_applied
    )
    return mixed * math.sqrt(C)


def solution(mesh):
    grid = Mesh(mesh.devices.reshape(8, 2, 2, 2, 4), ("z", "x_hi", "core", "x_lo", "y"))
    spec = P(TP, ("z", "x_hi", "core"))
    return jax.shard_map(local, mesh=grid, in_specs=(spec,), out_specs=spec, check_vma=False)
```

```python
import math

import jax
import jax.numpy as jnp
from jax import lax
from jax.sharding import Mesh, PartitionSpec as P

C = 18432


quintic_one = 3.4445
quintic_three = -4.775
quintic_five = 2.0315

TP = ("x_lo", "y")
SWAP = [(0, 1), (1, 0)]


def dot(a, b, dims):
    return lax.dot_general(a, b, (dims, ((), ())), preferred_element_type=jnp.float32)


def shift(v, axis, size, by):
    return lax.ppermute(v, axis, [(i, (i + by) % size) for i in range(size)])


def swap(v, axis):
    return lax.ppermute(v, axis, SWAP)


def rows_of(v, start, size):
    return lax.dynamic_slice_in_dim(v, start, size, 0)


def gather_tp(v, core, early_work=None):
    n = v.shape[0] // 2
    h = n // 2
    wave = (swap(v, "x_lo"), shift(v, "y", 4, 1), shift(v, "y", 4, -1))
    blocks = (v,) + lax.optimization_barrier(wave)
    first, f_x, f_left, f_right = (rows_of(w, core * n, n) for w in blocks)
    second, s_x, s_left, s_right = (rows_of(w, (1 - core) * n, n) for w in blocks)
    early = (
        jnp.concatenate([first, f_x, f_left, f_right], axis=0),
        jnp.concatenate([second, s_x, s_left, s_right], axis=0),
    )
    wave = (
        shift(jnp.concatenate([f_x, s_left[:h]], axis=0), "y", 4, 1),
        shift(jnp.concatenate([f_x, s_right[h:]], axis=0), "y", 4, -1),
        swap(s_left, "x_lo"),
    )
    done = early_work(early) if early_work is not None else early
    (to_right, to_left, sx_left), done = lax.optimization_barrier((wave, done))
    fx_left, far_low = to_right[:n], to_right[n:]
    fx_right, far_high = to_left[:n], to_left[n:]
    sx_right = swap(s_right, "x_lo")
    s_far = jnp.concatenate([far_low, far_high], axis=0)
    f_far = shift(f_left, "y", 4, 1)
    fx_far = shift(fx_right, "y", 4, -1)
    sx_far = swap(s_far, "x_lo")
    late = (
        jnp.concatenate([fx_left, f_far, fx_right, fx_far], axis=0),
        jnp.concatenate([sx_left, s_far, sx_right, sx_far], axis=0),
    )
    return early, late, done


def gather_z(v, base):
    rows, columns = v.shape
    h = columns // 2
    z = lax.axis_index("z")
    r1 = shift(v, "z", 8, 1)
    l1 = shift(v, "z", 8, -1)
    r2 = shift(r1, "z", 8, 1)
    l2 = shift(l1, "z", 8, -1)
    r3 = shift(r1, "z", 8, 2)
    l3 = shift(l1, "z", 8, -2)
    far = jnp.concatenate([shift(r2[:, :h], "z", 8, 2), shift(l2[:, h:], "z", 8, -2)], axis=1)
    out = base
    for by, piece in ((0, v), (-1, r1), (1, l1), (-2, r2), (2, l2), (-3, r3), (3, l3), (4, far)):
        out = lax.dynamic_update_slice_in_dim(out, piece, lax.rem(z + by + 8, 8) * rows, 0)
    return out


def low(v):
    return v.astype(jnp.bfloat16)


def wide(v):
    return v.astype(jnp.float32)


def local(x):
    core = lax.axis_index("core")

    def pair_sum(blocks):
        mine, other = blocks
        got = swap(low(dot(x, other, ((1,), (1,)))), "core")
        pair = low(dot(x, mine, ((1,), (1,))) + wide(got))
        return pair.reshape(8, pair.shape[0] // 8, pair.shape[1])

    def exchange_z(pair):
        return lax.all_to_all(pair, "z", 0, 0)

    def finish(split):
        plane = low(jnp.sum(wide(split), axis=0))
        return low(wide(plane) + wide(swap(plane, "x_hi")))

    *parts, pair = gather_tp(x, core, pair_sum)
    sent = exchange_z(pair)
    sent, pair = lax.optimization_barrier((sent, pair_sum(parts[1])))
    rows = [finish(sent), finish(exchange_z(pair))]
    rows = jnp.concatenate(rows, axis=1)
    gram_mine = gather_z(rows, jnp.zeros((8 * rows.shape[0], rows.shape[1]), rows.dtype))
    gram_other = swap(gram_mine, "core")
    n = rows.shape[1] // 2
    grams = [g[:, i : i + n] for i in (0, n) for g in (gram_mine, gram_other)]

    def apply(blocks, order):
        flat = [b for part in blocks for b in part]
        total = 0
        for i in order:
            total = total + dot(grams[i], flat[i], ((1,), (0,)))
        return total

    applied = apply(parts, (0, 2, 1, 3))
    twice_applied = apply(gather_tp(low(applied), core)[:2], (0, 1, 2, 3))
    mixed = (
        quintic_one * x.astype(jnp.float32)
        + quintic_three * applied
        + quintic_five * twice_applied
    )
    return mixed * math.sqrt(C)


def solution(mesh):
    grid = Mesh(mesh.devices.reshape(8, 2, 2, 2, 4), ("z", "x_hi", "core", "x_lo", "y"))
    spec = P(TP, ("z", "x_hi", "core"))
    return jax.shard_map(local, mesh=grid, in_specs=(spec,), out_specs=spec, check_vma=False)
```

```python
import math

import jax
import jax.numpy as jnp
from jax import lax
from jax.sharding import Mesh, PartitionSpec as P

C = 18432


quintic_one = 3.4445
quintic_three = -4.775
quintic_five = 2.0315

TP = ("x_lo", "y")
SWAP = [(0, 1), (1, 0)]


def dot(a, b, dims):
    return lax.dot_general(a, b, (dims, ((), ())), preferred_element_type=jnp.float32)


def shift(v, axis, size, by):
    return lax.ppermute(v, axis, [(i, (i + by) % size) for i in range(size)])


def swap(v, axis):
    return lax.ppermute(v, axis, SWAP)


def gather_tp(first, second, early_work=None):
    n = first.shape[0]
    h = n // 2
    whole = jnp.concatenate([first, second], axis=0)
    wave = (swap(whole, "x_lo"), shift(whole, "y", 4, 1), shift(whole, "y", 4, -1))
    (f_x, s_x), (f_left, s_left), (f_right, s_right) = (
        (v[:n], v[n:]) for v in lax.optimization_barrier(wave)
    )
    early = (
        jnp.concatenate([first, f_x, f_left, f_right], axis=0),
        jnp.concatenate([second, s_x, s_left, s_right], axis=0),
    )
    wave = (
        shift(jnp.concatenate([f_x, s_left[:h]], axis=0), "y", 4, 1),
        shift(jnp.concatenate([f_x, s_right[h:]], axis=0), "y", 4, -1),
        swap(s_left, "x_lo"),
    )
    done = early_work(early) if early_work is not None else early
    (to_right, to_left, sx_left), done = lax.optimization_barrier((wave, done))
    fx_left, far_low = to_right[:n], to_right[n:]
    fx_right, far_high = to_left[:n], to_left[n:]
    sx_right = swap(s_right, "x_lo")
    s_far = jnp.concatenate([far_low, far_high], axis=0)
    f_far = shift(f_left, "y", 4, 1)
    fx_far = shift(fx_right, "y", 4, -1)
    sx_far = swap(s_far, "x_lo")
    late = (
        jnp.concatenate([fx_left, f_far, fx_right, fx_far], axis=0),
        jnp.concatenate([sx_left, s_far, sx_right, sx_far], axis=0),
    )
    return early, late, done


def gather_z(v, base):
    rows, columns = v.shape
    h = columns // 2
    z = lax.axis_index("z")
    r1 = shift(v, "z", 8, 1)
    l1 = shift(v, "z", 8, -1)
    r2 = shift(r1, "z", 8, 1)
    l2 = shift(l1, "z", 8, -1)
    r3 = shift(r1, "z", 8, 2)
    l3 = shift(l1, "z", 8, -2)
    far = jnp.concatenate([shift(r2[:, :h], "z", 8, 2), shift(l2[:, h:], "z", 8, -2)], axis=1)
    out = base
    for by, piece in ((0, v), (-1, r1), (1, l1), (-2, r2), (2, l2), (-3, r3), (3, l3), (4, far)):
        out = lax.dynamic_update_slice_in_dim(out, piece, lax.rem(z + by + 8, 8) * rows, 0)
    return out


def halves(v, core):
    half = v.shape[0] // 2
    return (
        lax.dynamic_slice_in_dim(v, core * half, half, 0),
        lax.dynamic_slice_in_dim(v, (1 - core) * half, half, 0),
    )


def low(v):
    return v.astype(jnp.bfloat16)


def wide(v):
    return v.astype(jnp.float32)


def local(x):
    core = lax.axis_index("core")

    def pair_sum(blocks):
        mine, other = blocks
        got = swap(low(dot(x, other, ((1,), (1,)))), "core")
        pair = low(dot(x, mine, ((1,), (1,))) + wide(got))
        return pair.reshape(8, pair.shape[0] // 8, pair.shape[1])

    def exchange_z(pair):
        return lax.all_to_all(pair, "z", 0, 0)

    def finish(split):
        plane = low(jnp.sum(wide(split), axis=0))
        return low(wide(plane) + wide(swap(plane, "x_hi")))

    *parts, pair = gather_tp(*halves(x, core), pair_sum)
    sent = exchange_z(pair)
    sent, pair = lax.optimization_barrier((sent, pair_sum(parts[1])))
    rows = [finish(sent), finish(exchange_z(pair))]
    rows = jnp.concatenate(rows, axis=1)
    gram_mine = gather_z(rows, jnp.zeros((8 * rows.shape[0], rows.shape[1]), rows.dtype))
    gram_other = swap(gram_mine, "core")
    n = rows.shape[1] // 2
    grams = [g[:, i : i + n] for i in (0, n) for g in (gram_mine, gram_other)]

    def apply(total, flat, order):
        for i in order:
            total = total + dot(grams[i], flat[i], ((1,), (0,)))
        return total

    applied = apply(0, parts[0] + parts[1], (0, 2, 1, 3))
    early, late, partial_sum = gather_tp(
        *halves(low(applied), core), lambda early: apply(0, early, (0, 1))
    )
    twice_applied = apply(partial_sum, early + late, (2, 3))
    mixed = (
        quintic_one * x.astype(jnp.float32)
        + quintic_three * applied
        + quintic_five * twice_applied
    )
    return mixed * math.sqrt(C)


def solution(mesh):
    grid = Mesh(mesh.devices.reshape(8, 2, 2, 2, 4), ("z", "x_hi", "core", "x_lo", "y"))
    spec = P(TP, ("z", "x_hi", "core"))
    return jax.shard_map(local, mesh=grid, in_specs=(spec,), out_specs=spec, check_vma=False)
```

```python
import math

import jax
import jax.numpy as jnp
from jax import lax
from jax.sharding import Mesh, PartitionSpec as P

C = 18432


quintic_one = 3.4445
quintic_three = -4.775
quintic_five = 2.0315

TP = ("x_lo", "y")
SWAP = [(0, 1), (1, 0)]


def dot(a, b, dims):
    return lax.dot_general(a, b, (dims, ((), ())), preferred_element_type=jnp.float32)


def shift(v, axis, size, by):
    return lax.ppermute(v, axis, [(i, (i + by) % size) for i in range(size)])


def swap(v, axis):
    return lax.ppermute(v, axis, SWAP)


def gather_tp(first, second, early_work=None):
    n = first.shape[0]
    h = n // 2
    whole = jnp.concatenate([first, second], axis=0)
    wave = (swap(whole, "x_lo"), shift(whole, "y", 4, 1), shift(whole, "y", 4, -1))
    (f_x, s_x), (f_left, s_left), (f_right, s_right) = (
        (v[:n], v[n:]) for v in lax.optimization_barrier(wave)
    )
    early = (
        jnp.concatenate([first, f_x, f_left, f_right], axis=0),
        jnp.concatenate([second, s_x, s_left, s_right], axis=0),
    )
    wave = (
        shift(jnp.concatenate([f_x, s_left[:h]], axis=0), "y", 4, 1),
        shift(jnp.concatenate([f_x, s_right[h:]], axis=0), "y", 4, -1),
        swap(s_left, "x_lo"),
    )
    done = early_work(early) if early_work is not None else early
    (to_right, to_left, sx_left), done = lax.optimization_barrier((wave, done))
    fx_left, far_low = to_right[:n], to_right[n:]
    fx_right, far_high = to_left[:n], to_left[n:]
    sx_right = swap(s_right, "x_lo")
    s_far = jnp.concatenate([far_low, far_high], axis=0)
    f_far = shift(f_left, "y", 4, 1)
    fx_far = shift(fx_right, "y", 4, -1)
    sx_far = swap(s_far, "x_lo")
    late = (
        jnp.concatenate([fx_left, f_far, fx_right, fx_far], axis=0),
        jnp.concatenate([sx_left, s_far, sx_right, sx_far], axis=0),
    )
    return early, late, done


def gather_z(parts, base):
    v = jnp.concatenate(parts, axis=1)
    rows, columns = v.shape
    h = columns // 2
    z = lax.axis_index("z")
    r1 = jnp.concatenate([shift(p, "z", 8, 1) for p in parts], axis=1)
    l1 = jnp.concatenate([shift(p, "z", 8, -1) for p in parts], axis=1)
    r2 = shift(r1, "z", 8, 1)
    l2 = shift(l1, "z", 8, -1)
    r3 = shift(r1, "z", 8, 2)
    l3 = shift(l1, "z", 8, -2)
    far = jnp.concatenate([shift(r2[:, :h], "z", 8, 2), shift(l2[:, h:], "z", 8, -2)], axis=1)
    out = base
    for by, piece in ((0, v), (-1, r1), (1, l1), (-2, r2), (2, l2), (-3, r3), (3, l3), (4, far)):
        out = lax.dynamic_update_slice_in_dim(out, piece, lax.rem(z + by + 8, 8) * rows, 0)
    return out


def halves(v, core):
    half = v.shape[0] // 2
    return (
        lax.dynamic_slice_in_dim(v, core * half, half, 0),
        lax.dynamic_slice_in_dim(v, (1 - core) * half, half, 0),
    )


def low(v):
    return v.astype(jnp.bfloat16)


def wide(v):
    return v.astype(jnp.float32)


def local(x):
    core = lax.axis_index("core")

    def pair_sum(blocks):
        mine, other = blocks
        got = swap(low(dot(x, other, ((1,), (1,)))), "core")
        pair = low(dot(x, mine, ((1,), (1,))) + wide(got))
        return pair.reshape(8, pair.shape[0] // 8, pair.shape[1])

    def exchange_z(pair):
        return lax.all_to_all(pair, "z", 0, 0)

    def finish(split):
        plane = low(jnp.sum(wide(split), axis=0))
        return low(wide(plane) + wide(swap(plane, "x_hi")))

    *parts, pair = gather_tp(*halves(x, core), pair_sum)
    sent = exchange_z(pair)
    sent, pair = lax.optimization_barrier((sent, pair_sum(parts[1])))
    rows = [finish(sent), finish(exchange_z(pair))]
    n = rows[0].shape[1]
    gram_mine = gather_z(rows, jnp.zeros((8 * rows[0].shape[0], 2 * n), rows[0].dtype))
    gram_other = swap(gram_mine, "core")
    grams = [g[:, i : i + n] for i in (0, n) for g in (gram_mine, gram_other)]

    def apply(blocks, order):
        flat = [b for part in blocks for b in part]
        total = 0
        for i in order:
            total = total + dot(grams[i], flat[i], ((1,), (0,)))
        return total

    applied = apply(parts, (0, 2, 1, 3))
    twice_applied = apply(gather_tp(*halves(low(applied), core))[:2], (0, 1, 2, 3))
    mixed = (
        quintic_one * x.astype(jnp.float32)
        + quintic_three * applied
        + quintic_five * twice_applied
    )
    return mixed * math.sqrt(C)


def solution(mesh):
    grid = Mesh(mesh.devices.reshape(8, 2, 2, 2, 4), ("z", "x_hi", "core", "x_lo", "y"))
    spec = P(TP, ("z", "x_hi", "core"))
    return jax.shard_map(local, mesh=grid, in_specs=(spec,), out_specs=spec, check_vma=False)
```
